32 devices in a mesh: cables: 2 (over x), chan: 16 (over z, y, core).
Axes of the slice: x: 2, y: 2, z: 4, core: 2. Of those that a mesh axis runs over, the one named last changes fastest.
Arguments:
- traces: bfloat16 [4096, 128], P(('cables', 'chan')), parts along dimension 0, may hold values from -30 to 30
- filter_coefs: float32 [16, 5], replicated, may hold values from -2 to 2, as said below
- leakage: bfloat16 [4096, 16], P(('cables', 'chan')), parts along dimension 0, may hold values from 0 to 1
- live_mask: int32 [4096], P(('cables', 'chan')), parts along dimension 0, may hold values 0 or 1
- aperture_starts: int32 [32], P(('cables', 'chan')), parts along dimension 0, may hold values from 0 to 2047, as said below
- delays: int32 [256, 512], replicated, may hold values from 0 to 15
- refine_lists: int32 [32, 2, 8], P(('cables', 'chan')), parts along dimension 0, may hold values from 0 to 255
Outputs:
- beam_power: bfloat16 [32, 256, 16, 128], P(('cables', 'chan')), parts along dimension 0
- refined_power: bfloat16 [32, 2, 8, 16, 128], P(('cables', 'chan')), parts along dimension 0
The draws below stay inside these ranges and needn't reach their ends.
There are 2 independent parts, one for each index of `cables`. The reference program is written for one: setup_inputs(seed, part) draws one part's arguments, and reference() takes and returns one part's arrays. A program takes and returns all parts, laid end to end along the dimension named above; an argument that names none is the same for every part. Nothing has to cross between parts.
Inputs may be any that keep to these rules, and one draw needn't show every extreme that they name: `aperture_starts`: aperture a begins at one of the 128 channels of block a // 1 of the cable (channels (a) * 128 up to that plus 128 - 1). `filter_coefs`: each band is a stable bandpass biquad.
All inputs are finite; a program needn't handle non-finite values. No bound on the sum of `live_mask` on one device may be relied on, other than what follows from the above.
Results may differ from the reference program's by a relative error of at most 0.0065.
Values may be sent and summed in bfloat16 or wider, within the bound.
A program may use at most 192 MiB of HBM per device.

```python
import math
import jax
import jax.numpy as jnp
from jax import lax

CH_DEV = 128
NT = 128
NB = 16
NP = 256
AP = 512
DMAX = 16
R = 8
PASSES = 2
A_DEV = 1
FIBRE_TAPS = 2048
NA = 16


def draw_traces(key, part):
    key_gain, key_common, key_noise = jax.random.split(key, 3)
    low_end = math.log(0.3)
    gains = jnp.exp(jax.random.uniform(key_gain, (FIBRE_TAPS, 1), jnp.float32, low_end, math.log(3.0)))
    common = jax.random.normal(key_common, (1, NT), jnp.float32)
    jitter_noise = jax.random.normal(key_noise, (FIBRE_TAPS, NT), jnp.float32)
    return jnp.clip(gains * (common + jitter_noise), -30.0, 30.0).astype(jnp.bfloat16)


def draw_filter_coefs(key, part):
    key_freq, key_width = jax.random.split(key)
    centre = jnp.exp(jax.random.uniform(key_freq, (NB,), jnp.float32, math.log(0.01), math.log(0.25)))
    quality = jax.random.uniform(key_width, (NB,), jnp.float32, 0.7, 4.0)
    angular = 2.0 * math.pi * centre
    spread = jnp.sin(angular) / (2.0 * quality)
    leading = 1.0 + spread
    return jnp.stack([spread / leading, jnp.zeros_like(leading), -spread / leading, -2.0 * jnp.cos(angular) / leading, (1.0 - spread) / leading], axis=1).astype(jnp.float32)


def draw_leakage(key, part):
    random_seed_list = jax.random.split(key, 8)
    order = jax.random.permutation(random_seed_list[0], NB)
    fast_count = jax.random.randint(random_seed_list[1], (), NB // 4, NB // 2 + 1)
    is_fast = order < fast_count
    quick_rate = jnp.exp(jax.random.uniform(random_seed_list[2], (NB,), jnp.float32, math.log(1.0 / 50.0), math.log(1.0 / 30.0)))
    slow_rate = jax.random.uniform(random_seed_list[3], (NB,), jnp.float32, 0.2, 0.6) / FIBRE_TAPS
    background_speed = jnp.where(is_fast, quick_rate, slow_rate)
    device_factor = jnp.exp(jax.random.uniform(random_seed_list[4], (FIBRE_TAPS // CH_DEV,), jnp.float32, math.log(0.7), math.log(1.4)))
    tap_readings = device_factor[jnp.arange(FIBRE_TAPS) // CH_DEV][:, None]
    rough_guess = jnp.exp(jax.random.uniform(random_seed_list[5], (FIBRE_TAPS, NB), jnp.float32, math.log(0.8), math.log(1.25)))
    transient_start = jax.random.randint(random_seed_list[6], (2,), 0, FIBRE_TAPS)
    transient_duration = jax.random.uniform(random_seed_list[7], (2,), jnp.float32, math.log(1.0 / 0.8), math.log(1.0 / 0.6))
    transient_onsets = jnp.sum((jnp.arange(FIBRE_TAPS)[:, None] == transient_start[None]).astype(jnp.float32) * transient_duration[None], axis=1)
    return (background_speed[None] * tap_readings * rough_guess + transient_onsets[:, None]).astype(jnp.bfloat16)


def draw_aperture_starts(key, part):
    owners = jnp.arange(NA) // A_DEV
    return (owners * CH_DEV + jax.random.randint(key, (NA,), 0, CH_DEV)).astype(jnp.int32)


def set_ends(array, stream_key, smallest, largest):
    longest = array.shape.index(max(array.shape))
    spots = []
    for shift in (0, 1):
        where = [jax.random.randint(jax.random.fold_in(stream_key, axis), (), 0, length) for axis, length in enumerate(array.shape)]
        where[longest] = (where[longest] + shift) % array.shape[longest]
        spots.append(tuple(where))
    return array.at[spots[0]].set(smallest).at[spots[1]].set(largest)


def setup_inputs(seed: int = 0, part: int = 0) -> dict:
    keys = jax.random.split(jax.random.key(seed), 8)
    part_keys = jax.random.split(jax.random.fold_in(keys[7], part), 8)
    traces = draw_traces(jax.random.fold_in(jax.random.fold_in(keys[7], part), 71), part)
    filter_coefs = draw_filter_coefs(jax.random.fold_in(keys[7], 71), part)
    leakage = draw_leakage(jax.random.fold_in(jax.random.fold_in(keys[7], part), 71), part)
    live_mask = set_ends((jax.random.randint(part_keys[3], (FIBRE_TAPS,), 0, 8) < 7).astype(jnp.int32), jax.random.fold_in(part_keys[3], 1), 0, 1)
    aperture_starts = draw_aperture_starts(jax.random.fold_in(jax.random.fold_in(keys[7], part), 71), part)
    delays = set_ends(jax.random.randint(keys[5], (NP, AP), 0, DMAX), jax.random.fold_in(keys[5], 1), 0, DMAX - 1).astype(jnp.int32)
    refine_lists = set_ends(jax.random.randint(part_keys[6], (NA, PASSES, R), 0, NP), jax.random.fold_in(part_keys[6], 1), 0, NP - 1).astype(jnp.int32)
    return dict(traces=traces, filter_coefs=filter_coefs, leakage=leakage, live_mask=live_mask, aperture_starts=aperture_starts, delays=delays, refine_lists=refine_lists)


eps_norm = 1e-06

def hilbert_table(samples):
    indices = jnp.arange(samples)
    offset = (indices[None, :] - indices[:, None]) % samples
    is_odd = offset % 2 == 1
    phases = jnp.pi * offset.astype(jnp.float32) / samples
    divisor = jnp.where(is_odd, jnp.sin(phases), 1.0)
    return jnp.where(is_odd, 2.0 / samples * jnp.cos(phases) / divisor, 0.0).astype(jnp.float32)

def envelope_power(signal, hilbert):
    turned = jnp.dot(signal, hilbert, precision=lax.Precision.HIGHEST, preferred_element_type=jnp.float32)
    return (signal * signal + turned * turned).astype(jnp.bfloat16)

def reference(traces, filter_coefs, leakage, live_mask, aperture_starts, delays, refine_lists):
    chan_count, samples = traces.shape
    band_count = filter_coefs.shape[0]
    b_zero = filter_coefs[:, 0]
    b_one = filter_coefs[:, 1]
    b_two = filter_coefs[:, 2]
    a_one = filter_coefs[:, 3]
    a_two = filter_coefs[:, 4]
    signal = traces.astype(jnp.float32)

    def advance(carry_state, in_now):
        in_last, in_before, out_last, out_before = carry_state
        out_now = b_zero * in_now[:, None] + b_one * in_last[:, None] + b_two * in_before[:, None] - a_one * out_last - a_two * out_before
        return ((in_now, in_last, out_now, out_last), out_now)
    flat_zero = jnp.zeros((chan_count,), jnp.float32)
    band_zero = jnp.zeros((chan_count, band_count), jnp.float32)
    _, response = lax.scan(advance, (flat_zero, flat_zero, band_zero, band_zero), signal.T)
    live_flag = live_mask.astype(jnp.float32)
    filtered = (live_flag[:, None, None] * jnp.transpose(response, (1, 2, 0))).astype(jnp.bfloat16)
    filtered = lax.optimization_barrier(filtered).astype(jnp.float32)
    leak_rate = leakage.astype(jnp.float32)
    retention = jnp.exp(-leak_rate)
    inflow = -jnp.expm1(-leak_rate)

    def follow(running_mean, inputs):
        filtered_now, keep_now, inflow_now = inputs
        running_mean = keep_now[:, None] * running_mean + inflow_now[:, None] * filtered_now
        return (running_mean, running_mean)
    _, running_mean = lax.scan(follow, jnp.zeros((band_count, samples), jnp.float32), (filtered, retention, inflow))
    detrended = (live_flag[:, None, None] * (filtered - running_mean)).astype(jnp.bfloat16)
    aperture_len = delays.shape[1]
    slowness_count = delays.shape[0]
    detrended = jnp.concatenate([detrended, jnp.zeros((aperture_len, band_count, samples), jnp.bfloat16)], axis=0)
    live_wide = jnp.concatenate([live_flag, jnp.zeros((aperture_len,), jnp.float32)])
    hilbert = hilbert_table(samples)
    time_index = jnp.arange(samples)
    slot_count = refine_lists.shape[2]

    def one_aperture(aperture):
        first_chan = aperture_starts[aperture].astype(jnp.int32)
        window = lax.dynamic_slice_in_dim(detrended, first_chan, aperture_len, 0).astype(jnp.float32)
        live_window = lax.dynamic_slice_in_dim(live_wide, first_chan, aperture_len, 0)
        padded = jnp.concatenate([jnp.zeros_like(window), window], axis=2)

        def add_channel(summed, inputs):
            channel_row, shift_now = inputs
            lookup = samples - shift_now[:, None] + time_index[None]
            return (summed + channel_row[:, lookup], None)
        summed, _ = lax.scan(add_channel, jnp.zeros((band_count, slowness_count, samples), jnp.float32), (padded, delays.T))
        stacked = jnp.transpose(summed, (1, 0, 2)) / math.sqrt(aperture_len)
        beam_out = envelope_power(stacked.reshape(-1, samples), hilbert).reshape(stacked.shape)
        guide_trace = stacked[refine_lists[aperture, 0]]
        pass_powers = []
        for pass_index in range(refine_lists.shape[1]):
            chosen = delays[refine_lists[aperture, pass_index]]
            lookup = samples - chosen[:, :, None] + time_index[None, None]
            full_shape = (slot_count, aperture_len, band_count, samples)
            aligned = jnp.take_along_axis(jnp.broadcast_to(padded[None], (slot_count,) + padded.shape), jnp.broadcast_to(lookup[:, :, None, :], full_shape), axis=3)
            guide_b = lax.optimization_barrier(guide_trace.astype(jnp.bfloat16)).astype(jnp.float32)
            numerator = jnp.einsum('rkbt,rbt->rk', aligned, guide_b)
            energy = lax.optimization_barrier(jnp.sum(aligned * aligned, axis=(2, 3)))
            guide_norm = jnp.sqrt(lax.optimization_barrier(jnp.sum(guide_b * guide_b, axis=(1, 2))) + eps_norm)
            coherence = numerator / (jnp.sqrt(energy + eps_norm) * guide_norm[:, None])
            weight = (live_window[None] * (0.25 + jnp.maximum(coherence, 0.0))).astype(jnp.bfloat16)
            weight = lax.optimization_barrier(weight).astype(jnp.float32)
            refined = jnp.einsum('rk,rkbt->rbt', weight, aligned)
            refined = refined / jnp.sqrt(1.0 + lax.optimization_barrier(jnp.sum(weight * weight, axis=1)))[:, None, None]
            pass_powers.append(envelope_power(refined.reshape(-1, samples), hilbert).reshape(refined.shape))
            guide_trace = refined
        return (beam_out, jnp.stack(pass_powers))
    return lax.map(one_aperture, jnp.arange(aperture_starts.shape[0]))
```

```python
import functools
import math

import numpy as np

import jax
import jax.numpy as jnp
from jax import lax
from jax.experimental import pallas as pl
from jax.experimental.pallas import tpu as pltpu
from jax.sharding import PartitionSpec as P

DMAX = 16
LANES = 128
EPS = 1e-06
MESH = pl.DeviceIdType.MESH
VM = pl.BlockSpec(memory_space=pltpu.VMEM)
SM = pl.BlockSpec(memory_space=pltpu.SMEM)
HB = pl.BlockSpec(memory_space=pl.ANY)


def hilbert_parts(samples):
    index = np.arange(samples)
    offset = (index[:, None] - index[None, :]) % samples
    odd = offset % 2 == 1
    phase = np.pi * offset / samples
    table = np.where(odd, 2.0 / samples * np.cos(phase) / np.where(odd, np.sin(phase), 1.0), 0.0)
    table = table.astype(np.float32)
    high = table.astype(jnp.bfloat16)
    low = (table - high.astype(np.float32)).astype(jnp.bfloat16)
    return jnp.asarray(high), jnp.asarray(low)


def inflow_of(leak):
    series = leak * (1.0 - leak * (0.5 - leak * (1.0 / 6.0 - leak * (1.0 / 24.0 - leak * (
        1.0 / 120.0 - leak * (1.0 / 720.0 - leak * (1.0 / 5040.0)))))))
    return jnp.where(leak < 0.5, series, 1.0 - jnp.exp(-leak))


def own_block_kernel(start_ref, pack_ref, coef_ref, msg_ref, loc_ref, wide):
    bands = coef_ref.shape[0]
    samples = msg_ref.shape[1]
    chans = pack_ref.shape[0]
    wide[...] = pack_ref[...].astype(jnp.float32).T
    lane = lax.broadcasted_iota(jnp.int32, (bands, chans), 1)
    leak = wide[samples : samples + bands, :]
    live = wide[samples + bands : samples + bands + 1, :]
    keep = jnp.exp(-leak)
    inflow = inflow_of(leak)
    coefs = [jnp.broadcast_to(coef_ref[:, i : i + 1], (bands, chans)) for i in range(5)]

    def ends(keep, inflow):
        after = keep
        total = keep
        step = 1
        while step < chans:
            rolled = pltpu.roll(after, chans - step, 1)
            after = after * jnp.where(lane < chans - step, rolled, 1.0)
            total = total * pltpu.roll(total, step, 1)
            step *= 2
        behind = jnp.where(lane < chans - 1, pltpu.roll(after, chans - 1, 1), 1.0)
        return behind * inflow, total

    offset = start_ref[0]
    weight_end, total_end = ends(keep, inflow)
    inside = lane < offset
    weight_loc, total_loc = ends(jnp.where(inside, keep, 1.0), jnp.where(inside, inflow, 0.0))
    msg_ref[...] = jnp.zeros_like(msg_ref)
    loc_ref[...] = jnp.zeros_like(loc_ref)
    zero = leak * 0.0
    tile = msg_ref[0:bands, :]
    time = lax.broadcasted_iota(jnp.int32, (bands, samples), 1)

    def step(t, state):
        x1, x2, y1, y2, end, loc = state
        x = jnp.broadcast_to(wide[pl.ds(t, 1), :], (bands, chans))
        y = coefs[0] * x + coefs[1] * x1 + coefs[2] * x2 - coefs[3] * y1 - coefs[4] * y2
        f = (live * y).astype(jnp.bfloat16).astype(jnp.float32)
        here = time == t
        end = jnp.where(here, jnp.sum(weight_end * f, axis=1, keepdims=True), end)
        loc = jnp.where(here, jnp.sum(weight_loc * f, axis=1, keepdims=True), loc)
        return x, x1, y, y1, end, loc

    state = lax.fori_loop(0, samples, step, (zero, zero, zero, zero, tile, tile), unroll=4)
    msg_ref[0:bands, :] = state[4]
    msg_ref[bands : 2 * bands, :] = total_end
    loc_ref[0:bands, :] = state[5]
    loc_ref[bands : 2 * bands, :] = total_loc


def exchange_kernel(count, near, pack_ref, msg_ref, packs_ref, msgs_ref, s1, r1, s2, r2):
    me = lax.axis_index("chan")
    barrier = pltpu.get_barrier_semaphore()
    for i in range(1, count):
        pl.semaphore_signal(
            barrier, inc=1, device_id={"chan": lax.rem(me + i, count)}, device_id_type=MESH
        )
    pl.semaphore_wait(barrier, count - 1)
    copies = []
    for i in range(1, count):
        copies.append(
            pltpu.make_async_remote_copy(
                src_ref=msg_ref,
                dst_ref=msgs_ref.at[me],
                send_sem=s1.at[i],
                recv_sem=r1.at[i],
                device_id={"chan": lax.rem(me + i, count)},
                device_id_type=MESH,
            )
        )
        copies[-1].start()
        if i <= near:
            copies.append(
                pltpu.make_async_remote_copy(
                    src_ref=pack_ref,
                    dst_ref=packs_ref.at[i - 1],
                    send_sem=s2.at[i],
                    recv_sem=r2.at[i],
                    device_id={"chan": lax.rem(me + count - i, count)},
                    device_id_type=MESH,
                )
            )
            copies[-1].start()
    for copy in copies:
        copy.wait()


def main_kernel(
    dims, info_ref, lists_ref, pack_ref, packs_ref, msgs_ref, loc_ref, coef_ref, delays_ref, hh_ref, hl_ref,
    out_ref, out2_ref, rows, wide, tabs, xt, energy, snap, delt, acc, acc2,
):
    samples, bands, chans, aperture, near, count = dims
    blocks = aperture // chans
    me = info_ref[1]
    offset = info_ref[0]
    points = samples * bands
    lead = (DMAX - 1) * bands

    rows[0:chans, :] = pack_ref[...].astype(jnp.float32)
    for j in range(near):
        inside = jnp.where(me + j + 1 < count, 1.0, 0.0)
        rows[(j + 1) * chans : (j + 2) * chans, :] = packs_ref[j].astype(jnp.float32) * inside
    span = (near + 1) * chans
    wide[...] = pltpu.roll(rows[...].T, span - offset, 1)[:, :aperture]
    delt[...] = delays_ref[...].T

    def add_device(i, state):
        return msgs_ref[i, bands : 2 * bands, 0:1] * state + msgs_ref[i, 0:bands, :]

    incoming = lax.fori_loop(0, me, add_device, jnp.zeros((bands, samples), jnp.float32))
    incoming = loc_ref[bands : 2 * bands, 0:1] * incoming + loc_ref[0:bands, :]

    lane = lax.broadcasted_iota(jnp.int32, (bands, chans), 1)
    steps = []
    size = 1
    while size < chans:
        steps.append(size)
        size *= 2
    for j in range(blocks):
        cols = slice(j * chans, (j + 1) * chans)
        leak = wide[samples : samples + bands, cols]
        prod = jnp.exp(-leak)
        for n, size in enumerate(steps):
            tabs[n * bands : (n + 1) * bands, cols] = jnp.where(lane >= size, prod, 0.0)
            prod = prod * jnp.where(lane >= size, pltpu.roll(prod, size, 1), 1.0)
        n = len(steps)
        tabs[n * bands : (n + 1) * bands, cols] = prod
        tabs[(n + 1) * bands : (n + 2) * bands, cols] = jnp.broadcast_to(
            prod[:, chans - 1 : chans], (bands, chans)
        )
        tabs[(n + 2) * bands : (n + 3) * bands, cols] = inflow_of(leak)
    live = wide[samples + bands : samples + bands + 1, :]
    xt[0:lead, :] = jnp.zeros((lead, aperture), jnp.bfloat16)
    energy[...] = jnp.zeros_like(energy)
    coefs = [jnp.broadcast_to(coef_ref[:, i : i + 1], (bands, chans)) for i in range(5)]
    time = lax.broadcasted_iota(jnp.int32, (bands, samples), 1)

    def tab(n, j):
        return tabs[n * bands : (n + 1) * bands, j * chans : (j + 1) * chans]

    def filter_step(t, state):
        x1, x2, y1s, y2s = state
        x = jnp.broadcast_to(wide[pl.ds(t, 1), :], (bands, aperture))
        carry = jnp.broadcast_to(
            jnp.sum(jnp.where(time == t, incoming, 0.0), axis=1, keepdims=True), (bands, chans)
        )
        slot = pl.multiple_of(jnp.maximum(t - (samples - DMAX), 0) * bands, bands)
        row = pl.multiple_of(lead + t * bands, bands)
        ys = []
        for j in range(blocks):
            cols = slice(j * chans, (j + 1) * chans)
            y = (
                coefs[0] * x[:, cols]
                + coefs[1] * x1[:, cols]
                + coefs[2] * x2[:, cols]
                - coefs[3] * y1s[j]
                - coefs[4] * y2s[j]
            )
            ys.append(y)
            f = (live[:, cols] * y).astype(jnp.bfloat16).astype(jnp.float32)
            v = tab(len(steps) + 2, j) * f
            for n, size in enumerate(steps):
                v = v + tab(n, j) * pltpu.roll(v, size, 1)
            mean = v + tab(len(steps), j) * carry
            if j + 1 < blocks:
                last = jnp.broadcast_to(v[:, chans - 1 : chans], (bands, chans))
                carry = last + tab(len(steps) + 1, j) * carry
            d = (live[:, cols] * (f - mean)).astype(jnp.bfloat16)
            xt[pl.ds(row, bands), cols] = d
            df = d.astype(jnp.float32)
            e = energy[:, cols] + df * df
            energy[:, cols] = e
            snap[pl.ds(slot, bands), cols] = e
        return x, x1, tuple(ys), y1s

    zero_row = energy[...]
    zeros = tuple(energy[:, j * chans : (j + 1) * chans] for j in range(blocks))
    lax.fori_loop(0, samples, filter_step, (zero_row, zero_row, zeros, zeros), unroll=2)

    tiles = delays_ref.shape[0] // LANES
    for j in range(tiles):
        acc[j] = jnp.zeros((points, LANES), jnp.float32)

    def add_delay(d, _):
        picked = jnp.where(delt[...] == d, 1.0, 0.0).astype(jnp.bfloat16)
        window = xt[pl.ds(pl.multiple_of((DMAX - 1 - d) * bands, bands), points), :]
        part = jnp.dot(window, picked, preferred_element_type=jnp.float32)
        for j in range(tiles):
            acc[j] += part[:, j * LANES : (j + 1) * LANES]
        return 0

    lax.fori_loop(0, DMAX, add_delay, 0)
    scale = 1.0 / math.sqrt(aperture)
    slow = delays_ref.shape[0]
    passes, slots = lists_ref.shape
    slow_id = lax.broadcasted_iota(jnp.int32, (1, slow), 1)
    nt_dims = (((1,), (1,)), ((), ()))
    pad = jnp.zeros((slots, DMAX * bands), jnp.float32)
    length = points + DMAX * bands
    norms = [
        jnp.sum(snap[(DMAX - d) * bands - bands : (DMAX - d) * bands, :], axis=0, keepdims=True)
        for d in range(DMAX)
    ]
    onehot = jnp.concatenate(
        [jnp.where(slow_id == lists_ref[0, r], 1.0, 0.0) for r in range(slots)], axis=0
    ).astype(jnp.bfloat16)
    guide = lax.dot_general(
        onehot,
        jnp.concatenate([(acc[j] * scale).astype(jnp.bfloat16) for j in range(tiles)], axis=1),
        nt_dims,
        preferred_element_type=jnp.float32,
    )
    results = []
    for i in range(passes):
        chosen = jnp.concatenate(
            [delays_ref[pl.ds(lists_ref[i, r], 1), :] for r in range(slots)], axis=0
        )
        guide = guide.astype(jnp.bfloat16).astype(jnp.float32)
        padded = jnp.concatenate([guide, pad], axis=1)
        shifted = [padded[:, :points]] + [
            pltpu.roll(padded, length - d * bands, 1)[:, :points] for d in range(1, DMAX)
        ]
        shifted = jnp.concatenate(shifted, axis=0).astype(jnp.bfloat16)
        products = jnp.dot(shifted, xt[lead : lead + points, :], preferred_element_type=jnp.float32)
        numerator = jnp.zeros((slots, aperture), jnp.float32)
        strength = jnp.zeros((slots, aperture), jnp.float32)
        for d in range(DMAX):
            match = chosen == d
            numerator = numerator + jnp.where(match, products[d * slots : (d + 1) * slots, :], 0.0)
            strength = strength + jnp.where(match, norms[d], 0.0)
        guide_norm = jnp.sqrt(jnp.sum(guide * guide, axis=1, keepdims=True) + EPS)
        coherence = numerator / (jnp.sqrt(strength + EPS) * guide_norm)
        weight = (live * (0.25 + jnp.maximum(coherence, 0.0))).astype(jnp.bfloat16).astype(jnp.float32)
        spread = jnp.concatenate(
            [jnp.where(chosen == d, weight, 0.0) for d in range(DMAX)], axis=0
        ).astype(jnp.bfloat16)
        parts = lax.dot_general(
            spread, xt[lead : lead + points, :], nt_dims, preferred_element_type=jnp.float32
        )
        refined = parts[0:slots, :]
        for d in range(1, DMAX):
            part = jnp.concatenate([parts[d * slots : (d + 1) * slots, :], pad], axis=1)
            refined = refined + pltpu.roll(part, d * bands, 1)[:, :points]
        refined = refined / jnp.sqrt(1.0 + jnp.sum(weight * weight, axis=1, keepdims=True))
        results.append(refined)
        guide = refined
    total = passes * slots
    results.append(jnp.zeros((LANES - total, points), jnp.float32))
    acc2[...] = jnp.concatenate(results, axis=0).T

    def envelope(band, _):
        s = jnp.concatenate(
            [acc.at[j][pl.ds(band, samples, stride=bands), :] * scale for j in range(tiles)]
            + [acc2[pl.ds(band, samples, stride=bands), :]],
            axis=1,
        )
        high = s.astype(jnp.bfloat16)
        low = (s - high.astype(jnp.float32)).astype(jnp.bfloat16)
        turned = (
            jnp.dot(hh_ref[...], high, preferred_element_type=jnp.float32)
            + jnp.dot(hh_ref[...], low, preferred_element_type=jnp.float32)
            + jnp.dot(hl_ref[...], high, preferred_element_type=jnp.float32)
        )
        power = (s * s + turned * turned).T.astype(jnp.bfloat16)
        cols = pl.ds(pl.multiple_of(band * samples, samples), samples)
        out_ref[:, cols] = power[:slow, :]
        out2_ref[:, cols] = power[slow : slow + total, :]
        return 0

    lax.fori_loop(0, bands, envelope, 0)


def per_device(traces, filter_coefs, leakage, live_mask, aperture_starts, delays, refine_lists):
    chans, samples = traces.shape
    bands = filter_coefs.shape[0]
    slow, aperture = delays.shape
    near = (aperture + chans - 1) // chans
    count = lax.axis_size("chan")
    me = lax.axis_index("chan").astype(jnp.int32)
    passes, slots = refine_lists.shape[1:]
    offset = aperture_starts[0] - me * chans
    info = jnp.stack([offset, me])
    width = -(-(samples + bands + 1) // LANES) * LANES
    pack = jnp.concatenate(
        [
            traces,
            leakage,
            live_mask.astype(jnp.bfloat16)[:, None],
            jnp.zeros((chans, width - samples - bands - 1), jnp.bfloat16),
        ],
        axis=1,
    )
    f32 = jnp.float32
    msg, loc = pl.pallas_call(
        own_block_kernel,
        out_shape=(
            jax.ShapeDtypeStruct((2 * bands, samples), f32),
            jax.ShapeDtypeStruct((2 * bands, samples), f32),
        ),
        in_specs=[SM, VM, VM],
        out_specs=(VM, VM),
        scratch_shapes=[pltpu.VMEM((width, chans), f32)],
    )(info, pack, filter_coefs)
    dma = pltpu.SemaphoreType.DMA
    packs, msgs = pl.pallas_call(
        functools.partial(exchange_kernel, count, near),
        out_shape=(
            jax.ShapeDtypeStruct((near, chans, width), jnp.bfloat16),
            jax.ShapeDtypeStruct((count, 2 * bands, samples), f32),
        ),
        in_specs=[HB, HB],
        out_specs=(HB, HB),
        scratch_shapes=[dma((count,)), dma((count,)), dma((near + 1,)), dma((near + 1,))],
        compiler_params=pltpu.CompilerParams(collective_id=0, has_side_effects=True),
    )(pack, msg)
    points = samples * bands
    hh, hl = hilbert_parts(samples)
    levels = (chans - 1).bit_length() + 3
    beam, refined = pl.pallas_call(
        functools.partial(main_kernel, (samples, bands, chans, aperture, near, count)),
        out_shape=(
            jax.ShapeDtypeStruct((slow, bands * samples), jnp.bfloat16),
            jax.ShapeDtypeStruct((passes * slots, bands * samples), jnp.bfloat16),
        ),
        in_specs=[SM, SM] + [VM] * 8,
        out_specs=(VM, VM),
        scratch_shapes=[
            pltpu.VMEM(((near + 1) * chans, width), f32),
            pltpu.VMEM((width, aperture), f32),
            pltpu.VMEM((levels * bands, aperture), f32),
            pltpu.VMEM((points + (DMAX - 1) * bands, aperture), jnp.bfloat16),
            pltpu.VMEM((bands, aperture), f32),
            pltpu.VMEM((DMAX * bands, aperture), f32),
            pltpu.VMEM((aperture, slow), jnp.int32),
            pltpu.VMEM((slow // LANES, points, LANES), f32),
            pltpu.VMEM((points, LANES), f32),
        ],
        compiler_params=pltpu.CompilerParams(vmem_limit_bytes=48 * 1024 * 1024),
    )(info, refine_lists[0], pack, packs, msgs, loc, filter_coefs, delays, hh, hl)
    return (
        beam.reshape(1, slow, bands, samples),
        refined.reshape(1, passes, slots, bands, samples),
    )


def solution(mesh):
    return jax.shard_map(
        per_device,
        mesh=mesh,
        in_specs=(
            P(("cables", "chan"), None),
            P(),
            P(("cables", "chan"), None),
            P(("cables", "chan")),
            P(("cables", "chan")),
            P(),
            P(("cables", "chan"), None, None),
        ),
        out_specs=(
            P(("cables", "chan"), None, None, None),
            P(("cables", "chan"), None, None, None, None),
        ),
        check_vma=False,
    )
```
